32 devices in a mesh: ent: 8 (over z, x), qry: 4 (over y, core).
Axes of the slice: x: 2, y: 2, z: 4, core: 2. Of those that a mesh axis runs over, the one named last changes fastest.
Arguments:
- ent_feat: bfloat16 [64, 8192], P(None, 'ent'), may hold values from -6 to 6
- query_head: int32 [16], replicated, may hold values from 0 to 8191
- query_rel: int32 [16], replicated, may hold values from 0 to 821
- query_table: bfloat16 [822, 64], replicated, may hold values from -5 to 5
- rel_table: bfloat16 [3, 822, 64], replicated, may hold values from -5 to 5
- layer_weight: bfloat16 [3, 64, 64], replicated, may hold values from -0.75 to 0.75
- layer_bias: float32 [3, 64], replicated, may hold values from -5 to 5
- norm_gain: float32 [3, 64], replicated, may hold values from 0.5 to 1.5
- norm_shift: float32 [3, 64], replicated, may hold values from -3 to 3
- reg_blocks: int32 [640, 2], P('ent'), may hold values from 0 to 63, as said below
- reg_rel: int32 [640], P('ent'), may hold values from 0 to 821
- reg_mask: int32 [640, 128, 128], P('ent'), may hold values 0 or 1
- hin_blocks: int32 [192, 2], P('ent'), may hold values from 0 to 63, as said below
- hin_rel: int32 [192], P('ent'), may hold values from 0 to 821
- hin_mask: int32 [192, 128, 128], P('ent'), may hold values 0 or 1
- hout_blocks: int32 [192, 2], P('ent'), may hold values from 0 to 63, as said below
- hout_rel: int32 [192], P('ent'), may hold values from 0 to 821
- hout_mask: int32 [192, 128, 128], P('ent'), may hold values 0 or 1
- read_weight: bfloat16 [128, 64], replicated, may hold values from -0.5 to 0.5
- read_bias: float32 [64], replicated, may hold values from -5 to 5
- read_out: float32 [64], replicated, may hold values from -0.75 to 0.75
Outputs:
- scores: float32 [16, 8192], P(None, ('ent', 'qry'))
- hub_scores: float32 [16, 128], P('qry', 'ent')
The draws below stay inside these ranges and needn't reach their ends.
Inputs may be any that keep to these rules, and one draw needn't show every extreme that they name: `reg_blocks`: rows are grouped by 80 per index of ent. Column 0 is a block of that index's own 8 blocks; column 1 is a block of the same index's or an adjacent index's entities. `hin_blocks`: rows are grouped by 24 per index of ent. Column 0 is a hub block, below 1; column 1 is a block of that index's own entities. `hout_blocks`: rows are grouped by 24 per index of ent. Column 0 is a block of that index's own entities; column 1 is a hub block, below 1.
All inputs are finite; a program needn't handle non-finite values. No bound on the sum of `reg_mask` or of `hin_mask` or of `hout_mask` on one device may be relied on, other than what follows from the above.
Results may differ from the reference program's by a relative error of at most 0.0075.
Values may be sent and summed in bfloat16 or wider, within the bound.
No kernel may reach another device: no remote copies, remote signals or barrier semaphores. Data moves between devices by JAX's collectives and lax.ppermute only.
A program may use at most 128 MiB of HBM per device.

```python
import jax
import jax.numpy as jnp
from jax import lax

D = 64
RELS = 822
BLOCK = 128
LAYERS = 3
HIN_DEV = 24
HOUT_DEV = 24
QUERIES = 16
ENT = 8192
BLK_DEV = 8
ENT_BLOCKS = 64
TILES_DEV = 80
REG_TILES = 640
HIN_TILES = 192
HOUT_TILES = 192
HUBS = 128
HUB_BLOCKS = 1
N_ENT = 8


def draw_reg_blocks(key, part):
    key_target = jax.random.fold_in(key, 101)
    key_source = jax.random.fold_in(key, 102)
    tile_ids = jnp.arange(REG_TILES, dtype=jnp.int32)
    device = tile_ids // TILES_DEV
    position = tile_ids % TILES_DEV
    target = jax.random.randint(key_target, (REG_TILES,), 0, BLK_DEV, dtype=jnp.int32)
    target = jnp.where(position == 0, BLK_DEV - 1, jnp.where(position == 1, 0, target))
    target = device * BLK_DEV + target
    source = (device - 1) * BLK_DEV + jax.random.randint(key_source, (REG_TILES,), 0, 3 * BLK_DEV, dtype=jnp.int32)
    source = jnp.where(position == 0, (device + 2) * BLK_DEV - 1, jnp.where(position == 1, (device - 1) * BLK_DEV, source))
    source = jnp.where(source < 0, source + BLK_DEV, source)
    source = jnp.where(source >= ENT_BLOCKS, source - BLK_DEV, source)
    return jnp.stack([target, source], axis=1).astype(jnp.int32)


def draw_hin_blocks(key, part):
    key_target = jax.random.fold_in(key, 201)
    key_source = jax.random.fold_in(key, 202)
    tile_ids = jnp.arange(HIN_TILES, dtype=jnp.int32)
    device = tile_ids // HIN_DEV
    position = tile_ids % HIN_DEV
    target = jax.random.randint(key_target, (HIN_TILES,), 0, HUB_BLOCKS, dtype=jnp.int32)
    target = jnp.where(position == 0, HUB_BLOCKS - 1, jnp.where(position == 1, 0, target))
    source = jax.random.randint(key_source, (HIN_TILES,), 0, BLK_DEV, dtype=jnp.int32)
    source = device * BLK_DEV + jnp.where(position == 0, BLK_DEV - 1, source)
    return jnp.stack([target, source], axis=1).astype(jnp.int32)


def draw_hout_blocks(key, part):
    key_target = jax.random.fold_in(key, 301)
    key_source = jax.random.fold_in(key, 302)
    tile_ids = jnp.arange(HOUT_TILES, dtype=jnp.int32)
    device = tile_ids // HOUT_DEV
    position = tile_ids % HOUT_DEV
    target = jax.random.randint(key_target, (HOUT_TILES,), 0, BLK_DEV, dtype=jnp.int32)
    target = device * BLK_DEV + jnp.where(position == 0, BLK_DEV - 1, target)
    source = jax.random.randint(key_source, (HOUT_TILES,), 0, HUB_BLOCKS, dtype=jnp.int32)
    source = jnp.where(position == 0, HUB_BLOCKS - 1, jnp.where(position == 1, 0, source))
    return jnp.stack([target, source], axis=1).astype(jnp.int32)


def touch_ends(entries, own_key, least, high):
    index_at = [jax.random.randint(jax.random.fold_in(own_key, axis), (), 0, length) for axis, length in enumerate(entries.shape)]
    widest = entries.shape.index(max(entries.shape))
    neighbour = index_at[:widest] + [(index_at[widest] + 1) % entries.shape[widest]] + index_at[widest + 1:]
    return entries.at[tuple(index_at)].set(least).at[tuple(neighbour)].set(high)


def level_of(stream_key, extent, split, low, largest):
    def one(dim, shards_of):
        steps = jax.random.uniform(jax.random.fold_in(jax.random.fold_in(stream_key, 6), dim), (shards_of,), jnp.float32, low / len(split), largest / len(split))
        return jnp.repeat(jnp.exp(steps), extent[dim] // shards_of).reshape((-1,) + (1,) * (len(extent) - dim - 1))

    level = one(*split[0])
    for cut in split[1:]:
        level = level * one(*cut)
    return level


def centred(key, shape, deviation, reach, cuts=(), kind=jnp.bfloat16):
    factor_of = level_of(key, shape, cuts, -0.22, 0.18) if cuts else 1.0
    drawn = jax.random.normal(key, shape, jnp.float32) * deviation * factor_of
    return jnp.minimum(jnp.maximum(drawn, -reach), reach).astype(kind)


def setup_inputs(seed: int = 0) -> dict:
    keys = jax.random.split(jax.random.key(seed), 22)
    return {
        "ent_feat": centred(keys[0], (D, ENT), 1.0, 6.0, ((1, 8),)),
        "query_head": touch_ends(jax.random.randint(keys[1], (QUERIES,), 0, ENT), jax.random.fold_in(keys[1], 1), 0, ENT - 1).astype(jnp.int32),
        "query_rel": touch_ends(jax.random.randint(keys[2], (QUERIES,), 0, RELS), jax.random.fold_in(keys[2], 1), 0, RELS - 1).astype(jnp.int32),
        "query_table": centred(keys[3], (RELS, D), 1.0, 5.0),
        "rel_table": centred(keys[4], (LAYERS, RELS, D), 1.0, 5.0),
        "layer_weight": centred(keys[5], (LAYERS, D, D), D ** -0.5, 0.75),
        "layer_bias": centred(keys[6], (LAYERS, D), 1.0, 5.0, (), jnp.float32),
        "norm_gain": jnp.clip(1.0 + 0.1 * jax.random.normal(keys[7], (LAYERS, D), jnp.float32), 0.5, 1.5),
        "norm_shift": centred(keys[8], (LAYERS, D), 0.5, 3.0, (), jnp.float32),
        "reg_blocks": draw_reg_blocks(jax.random.fold_in(keys[21], 71), 0),
        "reg_rel": touch_ends(jax.random.randint(keys[10], (REG_TILES,), 0, RELS), jax.random.fold_in(keys[10], 1), 0, RELS - 1).astype(jnp.int32),
        "reg_mask": touch_ends((jax.random.randint(keys[11], (REG_TILES, BLOCK, BLOCK), 0, 16) < 1).astype(jnp.int32), jax.random.fold_in(keys[11], 1), 0, 1),
        "hin_blocks": draw_hin_blocks(jax.random.fold_in(keys[21], 71), 0),
        "hin_rel": touch_ends(jax.random.randint(keys[13], (HIN_TILES,), 0, RELS), jax.random.fold_in(keys[13], 1), 0, RELS - 1).astype(jnp.int32),
        "hin_mask": touch_ends((jax.random.randint(keys[14], (HIN_TILES, BLOCK, BLOCK), 0, 16) < 1).astype(jnp.int32), jax.random.fold_in(keys[14], 1), 0, 1),
        "hout_blocks": draw_hout_blocks(jax.random.fold_in(keys[21], 71), 0),
        "hout_rel": touch_ends(jax.random.randint(keys[16], (HOUT_TILES,), 0, RELS), jax.random.fold_in(keys[16], 1), 0, RELS - 1).astype(jnp.int32),
        "hout_mask": touch_ends((jax.random.randint(keys[17], (HOUT_TILES, BLOCK, BLOCK), 0, 16) < 1).astype(jnp.int32), jax.random.fold_in(keys[17], 1), 0, 1),
        "read_weight": centred(keys[18], (2 * D, D), (2 * D) ** -0.5, 0.5),
        "read_bias": centred(keys[19], (D,), 1.0, 5.0, (), jnp.float32),
        "read_out": centred(keys[20], (D,), D ** -0.5, 0.75, (), jnp.float32),
    }


def normalize(values, along_axis, gain_rows, shift_rows):
    average = lax.optimization_barrier(jnp.mean(values, axis=along_axis, keepdims=True))
    centered = values - average
    variance = lax.optimization_barrier(jnp.mean(centered * centered, axis=along_axis, keepdims=True))
    return centered * lax.rsqrt(variance + 1e-05) * gain_rows + shift_rows

def reference(ent_feat, query_head, query_rel, query_table, rel_table, layer_weight, layer_bias, norm_gain, norm_shift, reg_blocks, reg_rel, reg_mask, hin_blocks, hin_rel, hin_mask, hout_blocks, hout_rel, hout_mask, read_weight, read_bias, read_out):
    state_rows = QUERIES * D
    q_emb = query_table[query_rel].astype(jnp.float32)
    head_hits = (jnp.arange(ENT, dtype=jnp.int32)[None, :] == query_head[:, None]).astype(jnp.float32)
    boundary = q_emb[:, :, None] * head_hits[:, None, :]
    states = (ent_feat.astype(jnp.float32)[None] + boundary).astype(jnp.bfloat16)
    hub_states = jnp.zeros((HUBS, state_rows), jnp.bfloat16)
    per_device = (jnp.arange(N_ENT, dtype=jnp.int32), reg_blocks.reshape(N_ENT, TILES_DEV, 2), reg_rel.reshape(N_ENT, TILES_DEV), reg_mask.reshape(N_ENT, TILES_DEV, BLOCK, BLOCK), hin_blocks.reshape(N_ENT, HIN_DEV, 2), hin_rel.reshape(N_ENT, HIN_DEV), hin_mask.reshape(N_ENT, HIN_DEV, BLOCK, BLOCK), hout_blocks.reshape(N_ENT, HOUT_DEV, 2), hout_rel.reshape(N_ENT, HOUT_DEV), hout_mask.reshape(N_ENT, HOUT_DEV, BLOCK, BLOCK))
    highest = lax.Precision.HIGHEST
    for layer_at in range(LAYERS):
        coef_table = rel_table[layer_at].astype(jnp.float32)[None, :, :] * q_emb[:, None, :]
        state_blocks = states.reshape(state_rows, ENT_BLOCKS, BLOCK)
        hub_view = hub_states.reshape(HUB_BLOCKS, BLOCK, state_rows)

        def coefficients(rel_ids):
            return jnp.transpose(coef_table[:, rel_ids, :], (0, 2, 1)).reshape(state_rows, -1)

        def device_step(hub_carry, pieces):
            device, reg_pairs, reg_ids, reg_tiles, hin_pairs, hin_ids, hin_tiles, hout_pairs, hout_ids, hout_tiles = pieces
            first_block = device * BLK_DEV
            local_iota = jnp.arange(BLK_DEV, dtype=jnp.int32)[None, :]
            gathered = jnp.take(state_blocks, reg_pairs[:, 1], axis=1).astype(jnp.float32)
            product = jnp.einsum('ctj,tjk->ctk', gathered, reg_tiles.astype(jnp.float32), precision=highest)
            product = product * coefficients(reg_ids)[:, :, None]
            onehot = (reg_pairs[:, 0][:, None] - first_block == local_iota).astype(jnp.float32)
            totals = jnp.einsum('ctk,tb->cbk', product, onehot, precision=highest)
            hub_sources = jnp.take(hub_view, hout_pairs[:, 1], axis=0).astype(jnp.float32)
            product = jnp.einsum('tjc,tjk->ctk', hub_sources, hout_tiles.astype(jnp.float32), precision=highest)
            product = product * coefficients(hout_ids)[:, :, None]
            onehot = (hout_pairs[:, 0][:, None] - first_block == local_iota).astype(jnp.float32)
            totals = totals + jnp.einsum('ctk,tb->cbk', product, onehot, precision=highest)
            own = jnp.take(state_blocks, hin_pairs[:, 1], axis=1).astype(jnp.float32)
            hin_product = jnp.einsum('ctj,tjk->tkc', own, hin_tiles.astype(jnp.float32), precision=highest)
            hin_product = hin_product * coefficients(hin_ids).T[:, None, :]
            hub_onehot = (hin_pairs[:, 0][:, None] == jnp.arange(HUB_BLOCKS, dtype=jnp.int32)[None, :]).astype(jnp.float32)
            hub_carry = hub_carry + jnp.einsum('tkc,th->hkc', hin_product, hub_onehot, precision=highest)
            return (hub_carry, totals)
        hub_totals, totals = lax.scan(device_step, jnp.zeros((HUB_BLOCKS, BLOCK, state_rows), jnp.float32), per_device)
        totals = jnp.transpose(totals, (1, 0, 2, 3)).reshape(QUERIES, D, ENT)
        inputs = (totals + boundary).astype(jnp.bfloat16)
        weight = layer_weight[layer_at].astype(jnp.float32)
        linear = jnp.einsum('qdv,de->qev', inputs.astype(jnp.float32), weight) + layer_bias[layer_at][None, :, None]
        normed = normalize(linear, 1, norm_gain[layer_at][None, :, None], norm_shift[layer_at][None, :, None])
        hub_inputs = hub_totals.reshape(HUBS, QUERIES, D).astype(jnp.bfloat16)
        hub_linear = jnp.einsum('hqd,de->hqe', hub_inputs.astype(jnp.float32), weight) + layer_bias[layer_at][None, None, :]
        hub_normed = normalize(hub_linear, 2, norm_gain[layer_at][None, None, :], norm_shift[layer_at][None, None, :])
        states = (jax.nn.relu(normed) + states.astype(jnp.float32)).astype(jnp.bfloat16)
        hub_new = jax.nn.relu(hub_normed) + hub_states.astype(jnp.float32).reshape(HUBS, QUERIES, D)
        hub_states = hub_new.astype(jnp.bfloat16).reshape(HUBS, state_rows)
    query_part = jnp.dot(q_emb.astype(jnp.bfloat16), read_weight[D:], preferred_element_type=jnp.float32) + read_bias[None, :]
    read_states = read_weight[:D].astype(jnp.float32)
    features = jax.nn.relu(jnp.einsum('qdv,de->qev', states.astype(jnp.float32), read_states) + query_part[:, :, None])
    scores = jnp.einsum('qev,e->qv', features, read_out, precision=highest)
    hub_features = jax.nn.relu(jnp.einsum('hqd,de->hqe', hub_states.reshape(HUBS, QUERIES, D).astype(jnp.float32), read_states) + query_part[None])
    hub_scores = jnp.einsum('hqe,e->qh', hub_features, read_out, precision=highest)
    return (scores, hub_scores)
```

```python
import functools

import jax
import jax.numpy as jnp
from jax import lax
from jax.experimental import pallas as pl
from jax.experimental.pallas import tpu as pltpu
from jax.sharding import PartitionSpec as P

HUB_DEV = 16
JOIN = 4
F32 = jnp.float32
BF16 = jnp.bfloat16
SMEM = pl.BlockSpec(memory_space=pltpu.SMEM)
VMEM = pl.BlockSpec(memory_space=pltpu.VMEM)
LEFT, OWN, RIGHT, HOUT, HIN = range(5)


class Plan:
    def __init__(self, tiles, blocks, hub_blocks):
        self.tiles = tiles
        self.keys = 4 * blocks + hub_blocks
        self.chunks = tiles // JOIN + self.keys
        self.target = 8
        self.tile = self.target + self.chunks
        self.source = self.tile + self.chunks * JOIN
        self.size = self.source + self.chunks * JOIN


def prep_kernel(
    plan, blocks, hub_blocks, splits, layers,
    reg_blocks, hin_blocks, hout_blocks, reg_rel, hin_rel, hout_rel, query_rel, query_head,
    query_table, rel_table, read_weight, read_bias, reg_mask, hin_mask, hout_mask,
    turned, rel_rows, lane_rows, lane_heads, order, table, rows, q_rows, key_of, source_of, count_of, slot_of,
):
    step = pl.program_id(0)
    tiles_reg, tiles_hin = reg_rel.shape[0], hin_rel.shape[0]
    tiles_hout = hout_rel.shape[0]
    q_local, width = q_rows.shape[0] - 4, query_table.shape[1]
    lanes = lane_rows.shape[1]

    @pl.when(step == 0)
    def _():
        first_block = lax.axis_index("ent") * blocks
        query_first = lax.axis_index("qry") * q_local

        def clear(k, _):
            count_of[k] = 0
            return 0

        lax.fori_loop(0, plan.keys, clear, 0)

        def note(tile, key, source):
            key_of[tile] = key
            source_of[tile] = source
            count_of[key] = count_of[key] + 1

        def note_reg(t, _):
            place = reg_blocks[t, 1] - first_block + blocks
            side = lax.div(place, blocks)
            note(t, side * blocks + reg_blocks[t, 0] - first_block, place - side * blocks)
            return 0

        def note_hin(t, _):
            note(tiles_reg + t, 4 * blocks + hin_blocks[t, 0], hin_blocks[t, 1] - first_block)
            return 0

        def note_hout(t, _):
            note(
                tiles_reg + tiles_hin + t,
                3 * blocks + hout_blocks[t, 0] - first_block,
                hout_blocks[t, 1],
            )
            return 0

        lax.fori_loop(0, tiles_reg, note_reg, 0)
        lax.fori_loop(0, tiles_hin, note_hin, 0)
        lax.fori_loop(0, tiles_hout, note_hout, 0)

        chunk = jnp.int32(0)
        for side in range(5):
            order[side] = chunk
            keys = hub_blocks if side == HIN else blocks

            def lay(k, chunk, side=side):
                key = side * blocks + k
                slot_of[key] = chunk * JOIN
                need = lax.div(count_of[key] + (JOIN - 1), JOIN)

                def fill(c, _):
                    order[plan.target + c] = k
                    for u in range(JOIN):
                        order[plan.tile + c * JOIN + u] = plan.tiles
                        order[plan.source + c * JOIN + u] = 0
                    return 0

                lax.fori_loop(chunk, chunk + need, fill, 0)
                return chunk + need

            chunk = lax.fori_loop(0, keys, lay, chunk)
        order[5] = chunk

        def put(t, _):
            key = key_of[t]
            slot = slot_of[key]
            order[plan.tile + slot] = t
            order[plan.source + slot] = source_of[t]
            slot_of[key] = slot + 1
            return 0

        lax.fori_loop(0, plan.tiles, put, 0)

        table[...] = rel_table[...].astype(F32)
        rows[...] = jnp.zeros_like(rows)

        def rel_put(base, ref):
            def one(t, _):
                for layer in range(layers):
                    rows[layer, pl.ds(base + t, 1), :] = table[layer, pl.ds(ref[t], 1), :]
                return 0

            return one

        lax.fori_loop(0, tiles_reg, rel_put(0, reg_rel), 0)
        lax.fori_loop(0, tiles_hin, rel_put(tiles_reg, hin_rel), 0)
        lax.fori_loop(0, tiles_hout, rel_put(tiles_reg + tiles_hin, hout_rel), 0)
        spread = spreader(width, lanes)
        for layer in range(layers):
            rel_rows[layer] = jnp.dot(rows[layer].astype(BF16), spread, preferred_element_type=F32)

        table[0] = query_table[...].astype(F32)
        q_rows[...] = jnp.zeros_like(q_rows)
        for q in range(q_local):
            q_rows[pl.ds(q, 1), :] = table[0, pl.ds(query_rel[query_first + q], 1), :]
        own = q_rows[...].astype(BF16)
        parts = jnp.dot(own, read_weight[width:, :], preferred_element_type=F32) + read_bias[...]
        q_of_lane = lax.div(lax.broadcasted_iota(jnp.int32, (1, lanes), 1), width)
        values = jnp.dot(own, spread, preferred_element_type=F32)
        part_values = jnp.dot(parts, spread.astype(F32), precision=lax.Precision.HIGHEST)
        lane_q = jnp.zeros((1, lanes), F32)
        lane_part = jnp.zeros((1, lanes), F32)
        lane_head = jnp.zeros((1, lanes), jnp.int32)
        for q in range(q_local):
            lane_q = jnp.where(q_of_lane == q, values[q : q + 1, :], lane_q)
            lane_part = jnp.where(q_of_lane == q, part_values[q : q + 1, :], lane_part)
            lane_head = jnp.where(q_of_lane == q, query_head[query_first + q], lane_head)
        lane_rows[...] = jnp.zeros_like(lane_rows)
        lane_rows[0:1, :] = lane_q
        lane_rows[1:2, :] = lane_part
        lane_heads[...] = jnp.broadcast_to(lane_head, lane_heads.shape)

    def turn(mask):
        for t in range(mask.shape[0]):
            turned[t] = jnp.transpose(mask[t].astype(F32)).astype(BF16)

    pl.when(step < splits[0])(lambda: turn(reg_mask))
    pl.when((step >= splits[0]) & (step < splits[1]))(lambda: turn(hin_mask))
    pl.when(step >= splits[1])(lambda: turn(hout_mask))


def spreader(width, lanes):
    row = lax.broadcasted_iota(jnp.int32, (width, lanes), 0)
    column = lax.broadcasted_iota(jnp.int32, (width, lanes), 1)
    return (lax.rem(column, width) == row).astype(F32).astype(BF16)


def group_mean_matrix(width, lanes):
    row = lax.broadcasted_iota(jnp.int32, (lanes, lanes), 0)
    column = lax.broadcasted_iota(jnp.int32, (lanes, lanes), 1)
    same = lax.div(row, width) == lax.div(column, width)
    return jnp.where(same, 1.0 / width, 0.0).astype(BF16)


def split_dot(values, matrix):
    high = values.astype(BF16)
    low = (values - high.astype(F32)).astype(BF16)
    return jnp.dot(high, matrix, preferred_element_type=F32) + jnp.dot(
        low, matrix, preferred_element_type=F32
    )


def run_tiles(plan, side, order, turned, rel_row, source, total):
    block = turned.shape[1]
    lanes = total.shape[1]

    def chunk(c, _):
        masks, values = [], []
        for u in range(JOIN):
            tile = order[plan.tile + c * JOIN + u]
            start = pl.multiple_of(order[plan.source + c * JOIN + u] * block, block)
            row = jnp.broadcast_to(rel_row[pl.ds(tile, 1), :], (16, lanes)).astype(BF16)
            value = source[pl.ds(start, block), :].reshape(block // 16, 16, lanes)
            values.append((value * row[None]).reshape(block, lanes))
            masks.append(turned[jnp.minimum(tile, plan.tiles - 1)])
        product = jnp.dot(
            jnp.concatenate(masks, axis=1),
            jnp.concatenate(values, axis=0),
            preferred_element_type=F32,
        )
        place = pl.ds(pl.multiple_of(order[plan.target + c] * block, block), block)
        total[place, :] += product
        return 0

    lax.fori_loop(order[side], order[side + 1], chunk, 0)


def normed_step(inputs, weight, means, bias, gain, shift):
    linear = jnp.dot(inputs, weight, preferred_element_type=F32) + bias
    centered = linear - split_dot(linear, means)
    variance = split_dot(centered * centered, means)
    return jnp.maximum(centered * lax.rsqrt(variance + 1e-05) * gain + shift, 0.0)


def hit_lanes(rows, first, heads, values):
    place = first + lax.broadcasted_iota(jnp.int32, (rows, heads.shape[1]), 0)
    return jnp.where(place == heads, values, 0.0)


def first_states(feat, first, lane_rows, lane_heads, out):
    width, count = feat.shape
    lanes = out.shape[1]
    columns = jnp.transpose(feat[...].astype(F32)).astype(BF16)
    spread = spreader(width, lanes)
    block = 128
    for start in range(0, count, block):
        wide = jnp.dot(columns[start : start + block, :], spread, preferred_element_type=F32)
        hits = hit_lanes(block, first + start, lane_heads[0:1, :], lane_rows[0:1, :])
        out[start : start + block, :] = (wide + hits).astype(BF16)


def own_kernel(plan, layer, order, turned, rel_row, *refs):
    if layer == 0:
        feat, lane_rows, lane_heads, states, total, hub_part = refs
        first = lax.axis_index("ent") * feat.shape[1]
        first_states(feat, first, lane_rows, lane_heads, states)
    else:
        states, total, hub_part = refs
    hub_part[...] = jnp.zeros_like(hub_part)
    total[...] = jnp.zeros_like(total)
    run_tiles(plan, HIN, order, turned, rel_row, states, hub_part)
    run_tiles(plan, OWN, order, turned, rel_row, states, total)


def update_hubs(hub_sum, hub_old, lane_rows, params, weight, means, layer, layers):
    inputs = (hub_sum * lane_rows[0:1, :]).astype(BF16)
    grown = normed_step(
        inputs, weight, means, params[layer : layer + 1, :],
        params[layers + layer : layers + layer + 1, :],
        params[2 * layers + layer : 2 * layers + layer + 1, :],
    )
    if hub_old is None:
        return grown.astype(BF16)
    return (grown + hub_old.astype(F32)).astype(BF16)


def score_rows(values, weight, lane_part, picks):
    features = jnp.maximum(jnp.dot(values, weight, preferred_element_type=F32) + lane_part, 0.0)
    high = features.astype(BF16)
    low = (features - high.astype(F32)).astype(BF16)
    pick_high = picks.astype(BF16)
    pick_low = (picks - pick_high.astype(F32)).astype(BF16)

    def across(a, b):
        return lax.dot_general(a, b, (((1,), (1,)), ((), ())), preferred_element_type=F32)

    return across(pick_high, high) + across(pick_high, low) + across(pick_low, high)


def pick_matrix(read_row, width, lanes):
    row = lax.broadcasted_iota(jnp.int32, (8, lanes), 0)
    column = lax.broadcasted_iota(jnp.int32, (8, lanes), 1)
    return jnp.where(lax.div(column, width) == row, read_row, 0.0)


def close_kernel(plan, layer, layers, width, order, turned, rel_row, own, total_in, lane_rows, lane_heads, params, weights, *refs):
    last = layer == layers - 1
    lanes = own.shape[1]
    count = own.shape[0]
    first = lax.axis_index("ent") * count
    means = group_mean_matrix(width, lanes)
    if layer == 0:
        left_feat, right_feat, states, total, left, right = refs
        first_states(left_feat, first - count, lane_rows, lane_heads, left)
        first_states(right_feat, first + count, lane_rows, lane_heads, right)
        total[...] = total_in[...]
    else:
        if layer == 1:
            left, right, hub_sum, states, hub_new, total = refs
            hub_old = None
        else:
            left, right, hub_sum, hub_old_ref, states, hub_new, total = refs
            hub_old = hub_old_ref[...]
        hub_new[...] = update_hubs(
            hub_sum[...], hub_old, lane_rows, params, weights[layer - 1], means, layer - 1, layers
        )
        total[...] = total_in[...]
        run_tiles(plan, HOUT, order, turned, rel_row, hub_new, total)
    run_tiles(plan, LEFT, order, turned, rel_row, left, total)
    run_tiles(plan, RIGHT, order, turned, rel_row, right, total)
    weight = weights[layer]
    block = 128
    lane_q = lane_rows[0:1, :]
    for start in range(0, count, block):
        place = slice(start, start + block)
        hits = hit_lanes(block, first + start, lane_heads[0:1, :], lane_q)
        inputs = (total[place, :] * lane_q + hits).astype(BF16)
        grown = normed_step(
            inputs, weight, means, params[layer : layer + 1, :],
            params[layers + layer : layers + layer + 1, :],
            params[2 * layers + layer : 2 * layers + layer + 1, :],
        )
        new = (grown + own[place, :].astype(F32)).astype(BF16)
        if last:
            picks = pick_matrix(params[3 * layers : 3 * layers + 1, :], width, lanes)
            states[:, place] = score_rows(new, weights[layers], lane_rows[1:2, :], picks)
        else:
            states[place, :] = new


def hub_kernel(layers, width, hub_sum, hub_old, lane_rows, params, weights, out):
    lanes = hub_sum.shape[1]
    means = group_mean_matrix(width, lanes)
    new = update_hubs(
        hub_sum[...], hub_old[...], lane_rows, params, weights[layers - 1], means, layers - 1, layers
    )
    picks = pick_matrix(params[3 * layers : 3 * layers + 1, :], width, lanes)
    out[...] = score_rows(new, weights[layers], lane_rows[1:2, :], picks)


def body(
    ent_feat, query_head, query_rel, query_table, rel_table, layer_weight, layer_bias, norm_gain,
    norm_shift, reg_blocks, reg_rel, reg_mask, hin_blocks, hin_rel, hin_mask, hout_blocks,
    hout_rel, hout_mask, read_weight, read_bias, read_out,
):
    ends = lax.axis_size("ent")
    layers = rel_table.shape[0]
    q_local = query_head.shape[0] // lax.axis_size("qry")
    width, ent_local = ent_feat.shape
    block = reg_mask.shape[1]
    blocks = ent_local // block
    hubs = HUB_DEV * ends
    hub_blocks = hubs // block
    lanes = q_local * width
    counts = [reg_mask.shape[0], hin_mask.shape[0], hout_mask.shape[0]]
    tiles = sum(counts)
    plan = Plan(tiles, blocks, hub_blocks)
    padded = tiles + 8
    relations = rel_table.shape[1]

    group = 8
    while any(c % group for c in counts):
        group //= 2
    steps = [c // group for c in counts]
    splits = (steps[0], steps[0] + steps[1])

    def mask_spec(offset, length):
        return pl.BlockSpec(
            (group, block, block), lambda i: (jnp.clip(i - offset, 0, length - 1), 0, 0)
        )

    def whole(shape):
        return pl.BlockSpec(shape, lambda i: (0,) * len(shape))

    turned, rel_rows, lane_rows, lane_heads, order = pl.pallas_call(
        functools.partial(prep_kernel, plan, blocks, hub_blocks, splits, layers),
        grid=(sum(steps),),
        in_specs=[SMEM] * 8
        + [whole(query_table.shape), whole(rel_table.shape), whole(read_weight.shape), whole((1, width))]
        + [mask_spec(0, steps[0]), mask_spec(splits[0], steps[1]), mask_spec(splits[1], steps[2])],
        out_specs=[
            pl.BlockSpec((group, block, block), lambda i: (i, 0, 0)),
            whole((layers, padded, lanes)),
            whole((8, lanes)),
            whole((8, lanes)),
            SMEM,
        ],
        out_shape=[
            jax.ShapeDtypeStruct((tiles, block, block), BF16),
            jax.ShapeDtypeStruct((layers, padded, lanes), F32),
            jax.ShapeDtypeStruct((8, lanes), F32),
            jax.ShapeDtypeStruct((8, lanes), jnp.int32),
            jax.ShapeDtypeStruct((plan.size,), jnp.int32),
        ],
        scratch_shapes=[
            pltpu.VMEM((layers, relations, width), F32),
            pltpu.VMEM((layers, padded, width), F32),
            pltpu.VMEM((q_local + 4, width), F32),
            pltpu.SMEM((tiles,), jnp.int32),
            pltpu.SMEM((tiles,), jnp.int32),
            pltpu.SMEM((plan.keys,), jnp.int32),
            pltpu.SMEM((plan.keys,), jnp.int32),
        ],
        cost_estimate=pl.CostEstimate(
            flops=0, bytes_accessed=tiles * block * block * 6, transcendentals=0
        ),
        name="prep",
    )(
        reg_blocks, hin_blocks, hout_blocks, reg_rel, hin_rel, hout_rel, query_rel, query_head,
        query_table, rel_table, read_weight, read_bias[None, :], reg_mask, hin_mask, hout_mask,
    )

    params = jnp.tile(
        jnp.concatenate([layer_bias, norm_gain, norm_shift, read_out[None, :]], axis=0), (1, q_local)
    )
    same = jnp.arange(lanes)[:, None] // width == jnp.arange(lanes)[None, :] // width
    square = jnp.concatenate([layer_weight, read_weight[None, :width]], axis=0)
    weights = jnp.where(same[None], jnp.tile(square, (1, q_local, q_local)), jnp.zeros((), BF16))

    def shifts(cells):
        left = lax.ppermute(cells, "ent", [(i, i + 1) for i in range(ends - 1)])
        right = lax.ppermute(cells, "ent", [(i + 1, i) for i in range(ends - 1)])
        return left, right

    def summed(part):
        stride = 1
        while stride < ends:
            part = part + lax.ppermute(part, "ent", [(i, i ^ stride) for i in range(ends)])
            stride *= 2
        return part

    def call(kernel, name, operands, outs, scratch=(), tile_count=0):
        return pl.pallas_call(
            kernel,
            in_specs=[SMEM] + [VMEM] * (len(operands) - 1) if name != "hubs" else [VMEM] * len(operands),
            out_specs=[VMEM] * len(outs),
            out_shape=outs,
            scratch_shapes=list(scratch),
            cost_estimate=pl.CostEstimate(
                flops=2 * tile_count * block * block * lanes,
                bytes_accessed=4 * tile_count * block * block,
                transcendentals=0,
            ),
            name=name,
        )(*operands)

    state_shape = jax.ShapeDtypeStruct((ent_local, lanes), BF16)
    total_shape = jax.ShapeDtypeStruct((ent_local, lanes), F32)
    part_shape = jax.ShapeDtypeStruct((hubs, lanes), F32)
    hub_shape = jax.ShapeDtypeStruct((hubs, lanes), BF16)
    score_shape = jax.ShapeDtypeStruct((8, ent_local), F32)
    total_scratch = pltpu.VMEM((ent_local, lanes), F32)
    state_scratch = pltpu.VMEM((ent_local, lanes), BF16)

    left, right = shifts(ent_feat)
    states, total, part = call(
        functools.partial(own_kernel, plan, 0), "own",
        (order, turned, rel_rows[0], ent_feat, lane_rows, lane_heads),
        (state_shape, total_shape, part_shape), (), tiles // 2,
    )
    hub_old = None
    hub_sum = None
    for layer in range(layers):
        last = layer == layers - 1
        base = (order, turned, rel_rows[layer], states, total, lane_rows, lane_heads, params, weights)
        kernel = functools.partial(close_kernel, plan, layer, layers, width)
        next_sum = summed(part)
        out_shape = score_shape if last else state_shape
        if layer == 0:
            (states,) = call(
                kernel, "close", base + (left, right), (out_shape,),
                (total_scratch, state_scratch, state_scratch), tiles,
            )
        else:
            extra = (left, right, hub_sum) if layer == 1 else (left, right, hub_sum, hub_old)
            states, hub_old = call(
                kernel, "close", base + extra, (out_shape, hub_shape), (total_scratch,), tiles
            )
        hub_sum = next_sum
        if not last:
            left, right = shifts(states)
            total, part = call(
                functools.partial(own_kernel, plan, layer + 1), "own",
                (order, turned, rel_rows[layer + 1], states), (total_shape, part_shape), (), tiles // 2,
            )
    (hub_scores,) = call(
        functools.partial(hub_kernel, layers, width), "hubs",
        (hub_sum, hub_old, lane_rows, params, weights), (jax.ShapeDtypeStruct((8, hubs), F32),),
    )
    scores = lax.all_to_all(states[:q_local], "qry", split_axis=1, concat_axis=0, tiled=True)
    hub_scores = lax.dynamic_slice(
        hub_scores, (0, lax.axis_index("ent") * HUB_DEV), (q_local, HUB_DEV)
    )
    return scores, hub_scores


def solution(mesh):
    return jax.shard_map(
        body,
        mesh=mesh,
        in_specs=(
            P(None, "ent"), P(), P(), P(), P(), P(), P(), P(), P(),
            P("ent", None), P("ent"), P("ent", None, None),
            P("ent", None), P("ent"), P("ent", None, None),
            P("ent", None), P("ent"), P("ent", None, None),
            P(), P(), P(),
        ),
        out_specs=(P(None, ("ent", "qry")), P("qry", "ent")),
        check_vma=False,
    )
```

```python
import functools
import math

import jax
import jax.numpy as jnp
from jax import lax
from jax.experimental import pallas as pl
from jax.experimental.pallas import tpu as pltpu
from jax.sharding import PartitionSpec as P

HUB_DEV = 16
JOIN = 2
F32 = jnp.float32
BF16 = jnp.bfloat16
SMEM = pl.BlockSpec(memory_space=pltpu.SMEM)
VMEM = pl.BlockSpec(memory_space=pltpu.VMEM)
LEFT, OWN, RIGHT, HOUT, HIN = range(5)


class Plan:
    def __init__(self, counts, blocks, hub_blocks):
        reg, hin, hout = counts
        self.tiles = reg + hin + hout
        self.keys = [blocks, blocks, blocks, blocks, hub_blocks]
        mean = [reg / (3 * blocks)] * 3 + [hout / blocks, hin / hub_blocks]
        most = [reg] * 3 + [hout, hin]
        self.slots = [
            min(m + m % 2, 2 * math.ceil((a + 1.2 * math.sqrt(a)) / 2)) for a, m in zip(mean, most)
        ]
        self.first_key = [sum(self.keys[:s]) for s in range(5)]
        place = 16
        self.main = []
        for side in range(5):
            self.main.append(place)
            place += self.keys[side] * self.slots[side]
        self.target = []
        self.more = []
        for side in range(5):
            room = most[side] // JOIN + self.keys[side]
            self.target.append(place)
            self.more.append(place + room)
            place += room * (1 + JOIN)
        self.size = place


def spreader(width, lanes, transposed=False):
    shape = (lanes, width) if transposed else (width, lanes)
    row = lax.broadcasted_iota(jnp.int32, shape, 0)
    column = lax.broadcasted_iota(jnp.int32, shape, 1)
    hit = lax.rem(row, width) == column if transposed else lax.rem(column, width) == row
    return hit.astype(F32).astype(BF16)


def contract_last(a, b):
    return lax.dot_general(a, b, (((1,), (1,)), ((), ())), preferred_element_type=F32)


def prep_kernel(
    plan, blocks, splits, layers,
    reg_blocks, hin_blocks, hout_blocks, query_head, query_rel, reg_rel, hin_rel, hout_rel,
    query_table, rel_table, read_weight, read_bias, read_out, layer_weight, layer_bias, norm_gain,
    norm_shift, reg_mask, hin_mask, hout_mask,
    turned, rel_rows, lane_rows, lane_heads, weights, order, q_rows, count_of, chunk_of, used,
):
    step = pl.program_id(0)
    relations = query_table.shape[1]
    width = query_table.shape[0]
    lanes = lane_rows.shape[1]
    q_local = lanes // width
    block = turned.shape[1]

    @pl.when(step == 0)
    def _():
        first_block = lax.axis_index("ent") * blocks
        query_first = lax.axis_index("qry") * q_local
        for key in range(sum(plan.keys)):
            count_of[key] = 0
        for side in range(5):
            used[side] = 0
        empty = plan.tiles

        def clear(i, _):
            order[i] = empty
            return 0

        lax.fori_loop(plan.main[0], plan.target[0], clear, 0, unroll=8)

        def note(tile, side, local, source, slots, main, target, more, first_key):
            key = first_key + local
            seen = count_of[key]
            word = tile + source * 4096
            count_of[key] = seen + 1

            @pl.when(seen < slots)
            def _():
                order[main + local * slots + seen] = word

            @pl.when(seen >= slots)
            def _():
                over = seen - slots
                within = lax.rem(over, JOIN)

                @pl.when(within == 0)
                def _():
                    fresh = used[side]
                    used[side] = fresh + 1
                    chunk_of[key] = fresh
                    order[target + fresh] = local
                    for u in range(1, JOIN):
                        order[more + fresh * JOIN + u] = empty

                order[more + chunk_of[key] * JOIN + within] = word

        def pick(side, table):
            return jnp.where(side == 0, table[0], jnp.where(side == 1, table[1], table[2]))

        def note_reg(t, _):
            place = reg_blocks[1, t] - first_block + blocks
            side = lax.div(place, blocks)
            note(
                t, side, reg_blocks[0, t] - first_block, place - side * blocks, plan.slots[0],
                plan.main[0] + side * (plan.main[1] - plan.main[0]),
                plan.target[0] + side * (plan.target[1] - plan.target[0]),
                plan.more[0] + side * (plan.more[1] - plan.more[0]),
                side * blocks,
            )
            return 0

        def note_hin(t, _):
            note(
                reg_blocks.shape[1] + t, HIN, hin_blocks[0, t], hin_blocks[1, t] - first_block,
                plan.slots[HIN], plan.main[HIN], plan.target[HIN], plan.more[HIN], plan.first_key[HIN],
            )
            return 0

        def note_hout(t, _):
            note(
                reg_blocks.shape[1] + hin_blocks.shape[1] + t, HOUT, hout_blocks[0, t] - first_block,
                hout_blocks[1, t], plan.slots[HOUT], plan.main[HOUT], plan.target[HOUT],
                plan.more[HOUT], plan.first_key[HOUT],
            )
            return 0

        lax.fori_loop(0, reg_blocks.shape[1], note_reg, 0)
        lax.fori_loop(0, hin_blocks.shape[1], note_hin, 0)
        lax.fori_loop(0, hout_blocks.shape[1], note_hout, 0)
        for side in range(5):
            order[side] = used[side]

        spread = spreader(width, lanes)
        spread_back = spreader(width, lanes, True)

        def picked(table, ids):
            row = lax.broadcasted_iota(jnp.int32, (relations, ids.shape[1]), 0)
            hit = (row == ids[...]).astype(F32).astype(BF16)
            return jnp.transpose(jnp.dot(table, hit, preferred_element_type=F32))

        rel_rows[...] = jnp.zeros_like(rel_rows)
        base = 0
        for ids in (reg_rel, hin_rel, hout_rel):
            count = ids.shape[1]
            for layer in range(layers):
                rows = picked(rel_table[layer], ids)
                rel_rows[layer, base : base + count, :] = jnp.dot(
                    rows.astype(BF16), spread, preferred_element_type=F32
                )
            base += count

        q_rows[...] = picked(query_table[...], query_rel)
        q_of_lane = lax.div(lax.broadcasted_iota(jnp.int32, (1, lanes), 1), width)
        wide = jnp.dot(q_rows[...].astype(BF16), spread, preferred_element_type=F32)
        parts = contract_last(q_rows[...].astype(BF16), read_weight[:, width:]) + read_bias[...]

        def wide_rows(rows):
            return jnp.dot(rows, spread.astype(F32), precision=lax.Precision.HIGHEST)

        wide_parts = wide_rows(parts)
        query_at = lax.broadcasted_iota(jnp.int32, wide.shape, 0) - query_first
        mine = query_at == q_of_lane
        lane_rows[...] = jnp.zeros_like(lane_rows)
        lane_rows[0:1, :] = jnp.sum(jnp.where(mine, wide, 0.0), axis=0, keepdims=True)
        lane_rows[1:2, :] = jnp.sum(jnp.where(mine, wide_parts, 0.0), axis=0, keepdims=True)
        lane_rows[2:3, :] = wide_rows(read_out[...])
        for at, rows in ((3, layer_bias), (3 + layers, norm_gain), (3 + 2 * layers, norm_shift)):
            lane_rows[at : at + layers, :] = wide_rows(rows[...])
        lane_head = jnp.zeros((1, lanes), jnp.int32)
        for q in range(q_local):
            lane_head = jnp.where(q_of_lane == q, query_head[query_first + q], lane_head)
        lane_heads[...] = jnp.broadcast_to(lane_head, lane_heads.shape)

        same = lax.div(lax.broadcasted_iota(jnp.int32, (lanes, lanes), 0), width) == lax.div(
            lax.broadcasted_iota(jnp.int32, (lanes, lanes), 1), width
        )
        for layer in range(layers + 1):
            if layer < layers:
                tall = jnp.dot(spread_back, layer_weight[layer], preferred_element_type=F32)
            else:
                tall = contract_last(spread_back, read_weight[:, :width])
            full = jnp.dot(tall.astype(BF16), spread, preferred_element_type=F32)
            weights[layer] = jnp.where(same, full, 0.0).astype(BF16)
        weights[layers + 1] = jnp.where(same, 1.0 / width, 0.0).astype(BF16)

    def turn(mask):
        eye = lax.broadcasted_iota(jnp.int32, (block, block), 0) == lax.broadcasted_iota(
            jnp.int32, (block, block), 1
        )
        eye = eye.astype(F32).astype(BF16)
        for t in range(mask.shape[0]):
            turned[t] = contract_last(eye, mask[t].astype(F32).astype(BF16)).astype(BF16)

    pl.when(step < splits[0])(lambda: turn(reg_mask))
    pl.when((step >= splits[0]) & (step < splits[1]))(lambda: turn(hin_mask))
    pl.when(step >= splits[1])(lambda: turn(hout_mask))


def split_dot(values, matrix):
    high = values.astype(BF16)
    low = (values - high.astype(F32)).astype(BF16)
    return jnp.dot(high, matrix, preferred_element_type=F32) + jnp.dot(
        low, matrix, preferred_element_type=F32
    )


def slot_product(plan, layer, order, turned, rel_rows, places):
    block = turned.shape[1]
    lanes = rel_rows.shape[2]
    masks, values = [], []
    for place, source in places:
        word = order[place]
        tile = word & 4095
        start = pl.multiple_of((word >> 12) * block, block)
        row = jnp.broadcast_to(rel_rows[layer, pl.ds(tile, 1), :], (16, lanes)).astype(BF16)
        value = source[pl.ds(start, block), :].reshape(block // 16, 16, lanes)
        values.append((value * row[None]).reshape(block, lanes))
        masks.append(turned[jnp.where(tile == plan.tiles, 0, tile)])
    return jnp.dot(
        jnp.concatenate(masks, axis=1), jnp.concatenate(values, axis=0), preferred_element_type=F32
    )


def key_product(plan, layer, side_sources, key, order, turned, rel_rows):
    total = None
    for side, source in side_sources:
        slots = plan.slots[side]
        for start in range(0, slots, 6):
            places = [
                (plan.main[side] + key * slots + u, source) for u in range(start, min(start + 6, slots))
            ]
            product = slot_product(plan, layer, order, turned, rel_rows, places)
            total = product if total is None else total + product
    return total


def add_rest(plan, layer, side, source, order, turned, rel_rows, total):
    block = turned.shape[1]

    def chunk(c, _):
        places = [(plan.more[side] + c * JOIN + u, source) for u in range(JOIN)]
        place = pl.ds(pl.multiple_of(order[plan.target[side] + c] * block, block), block)
        total[place, :] += slot_product(plan, layer, order, turned, rel_rows, places)
        return 0

    lax.fori_loop(0, order[side], chunk, 0)


def normed_step(inputs, layer, layers, weights, lane_rows):
    means = weights[layers + 1]
    bias, gain, shift = (lane_rows[3 + layer + i * layers : 4 + layer + i * layers, :] for i in range(3))
    linear = jnp.dot(inputs, weights[layer], preferred_element_type=F32) + bias
    centered = linear - split_dot(linear, means)
    variance = split_dot(centered * centered, means)
    return jnp.maximum(centered * lax.rsqrt(variance + 1e-05) * gain + shift, 0.0)


def hit_lanes(rows, first, heads, values):
    place = first + lax.broadcasted_iota(jnp.int32, (rows, heads.shape[1]), 0)
    return jnp.where(place == heads, values, 0.0)


def first_states(feat, first, block, lane_rows, lane_heads, out):
    width, count = feat.shape
    columns = jnp.transpose(feat[...].astype(F32)).astype(BF16)
    spread = spreader(width, out.shape[1])
    for start in range(0, count, block):
        wide = jnp.dot(columns[start : start + block, :], spread, preferred_element_type=F32)
        hits = hit_lanes(block, first + start, lane_heads[0:1, :], lane_rows[0:1, :])
        out[start : start + block, :] = (wide + hits).astype(BF16)


def own_kernel(plan, layer, order, turned, rel_rows, *refs):
    block = turned.shape[1]
    if layer == 0:
        feat, lane_rows, lane_heads, states, total, hub_part = refs
        first = lax.axis_index("ent") * feat.shape[1]
        first_states(feat, first, block, lane_rows, lane_heads, states)
    else:
        states, total, hub_part = refs
    for side, out in ((HIN, hub_part), (OWN, total)):
        for key in range(plan.keys[side]):
            out[key * block : (key + 1) * block, :] = key_product(
                plan, layer, ((side, states),), key, order, turned, rel_rows
            )
        add_rest(plan, layer, side, states, order, turned, rel_rows, out)


def update_hubs(hub_sum, hub_old, layer, layers, weights, lane_rows):
    inputs = (hub_sum * lane_rows[0:1, :]).astype(BF16)
    grown = normed_step(inputs, layer, layers, weights, lane_rows)
    if hub_old is not None:
        grown = grown + hub_old.astype(F32)
    return grown.astype(BF16)


def hout_kernel(plan, layer, layers, order, turned, rel_rows, lane_rows, weights, total_in, hub_sum, *refs):
    block = turned.shape[1]
    if layer == 1:
        total, hub_new = refs
        hub_old = None
    else:
        old, total, hub_new = refs
        hub_old = old[...]
    hub_new[...] = update_hubs(hub_sum[...], hub_old, layer - 1, layers, weights, lane_rows)
    for key in range(plan.keys[HOUT]):
        place = slice(key * block, (key + 1) * block)
        total[place, :] = total_in[place, :] + key_product(
            plan, layer, ((HOUT, hub_new),), key, order, turned, rel_rows
        )
    add_rest(plan, layer, HOUT, hub_new, order, turned, rel_rows, total)


def score_rows(values, width, layers, weights, lane_rows):
    lanes = values.shape[1]
    row = lax.broadcasted_iota(jnp.int32, (8, lanes), 0)
    column = lax.broadcasted_iota(jnp.int32, (8, lanes), 1)
    picks = jnp.where(lax.div(column, width) == row, lane_rows[2:3, :], 0.0)
    features = jnp.dot(values, weights[layers], preferred_element_type=F32) + lane_rows[1:2, :]
    features = jnp.maximum(features, 0.0)
    high = features.astype(BF16)
    low = (features - high.astype(F32)).astype(BF16)
    pick_high = picks.astype(BF16)
    pick_low = (picks - pick_high.astype(F32)).astype(BF16)
    return contract_last(pick_high, high) + contract_last(pick_high, low) + contract_last(pick_low, high)


def close_kernel(plan, layer, layers, width, order, turned, rel_rows, lane_rows, lane_heads, weights, total_in, own, *refs):
    last = layer == layers - 1
    count = own.shape[0]
    block = turned.shape[1]
    first = lax.axis_index("ent") * count
    if layer == 0:
        left_feat, right_feat, out, total, left, right = refs
        first_states(left_feat, first - count, block, lane_rows, lane_heads, left)
        first_states(right_feat, first + count, block, lane_rows, lane_heads, right)
    else:
        left, right, out, total = refs
    total[...] = total_in[...]
    add_rest(plan, layer, LEFT, left, order, turned, rel_rows, total)
    add_rest(plan, layer, RIGHT, right, order, turned, rel_rows, total)
    lane_q = lane_rows[0:1, :]
    for key in range(plan.keys[LEFT]):
        place = slice(key * block, (key + 1) * block)
        sums = total[place, :] + key_product(
            plan, layer, ((LEFT, left), (RIGHT, right)), key, order, turned, rel_rows
        )
        hits = hit_lanes(block, first + key * block, lane_heads[0:1, :], lane_q)
        inputs = (sums * lane_q + hits).astype(BF16)
        grown = normed_step(inputs, layer, layers, weights, lane_rows)
        new = (grown + own[place, :].astype(F32)).astype(BF16)
        if last:
            out[:, place] = score_rows(new, width, layers, weights, lane_rows)[: out.shape[0]]
        else:
            out[place, :] = new


def hub_kernel(layers, width, lane_rows, weights, hub_sum, hub_old, out):
    mine = out.shape[1]
    place = pl.ds(pl.multiple_of(lax.axis_index("ent") * mine, mine), mine)
    new = update_hubs(hub_sum[place, :], hub_old[place, :], layers - 1, layers, weights, lane_rows)
    out[...] = score_rows(new, width, layers, weights, lane_rows)[: out.shape[0]]


def body(
    ent_feat, query_head, query_rel, query_table, rel_table, layer_weight, layer_bias, norm_gain,
    norm_shift, reg_blocks, reg_rel, reg_mask, hin_blocks, hin_rel, hin_mask, hout_blocks,
    hout_rel, hout_mask, read_weight, read_bias, read_out,
):
    ends = lax.axis_size("ent")
    layers = rel_table.shape[0]
    q_local = query_head.shape[0] // lax.axis_size("qry")
    width, ent_local = ent_feat.shape
    block = reg_mask.shape[1]
    blocks = ent_local // block
    hubs = HUB_DEV * ends
    lanes = q_local * width
    counts = [reg_mask.shape[0], hin_mask.shape[0], hout_mask.shape[0]]
    tiles = sum(counts)
    plan = Plan(counts, blocks, hubs // block)
    padded = tiles + 8
    queries = query_head.shape[0]

    group = 8
    while any(c % group for c in counts):
        group //= 2
    steps = [c // group for c in counts]
    splits = (steps[0], steps[0] + steps[1])

    def mask_spec(offset, length):
        return pl.BlockSpec(
            (group, block, block), lambda i: (jnp.clip(i - offset, 0, length - 1), 0, 0)
        )

    def whole(shape):
        return pl.BlockSpec(shape, lambda i: (0,) * len(shape))

    small = (
        query_rel[None, :], reg_rel[None, :], hin_rel[None, :], hout_rel[None, :],
        query_table.T, jnp.swapaxes(rel_table, 1, 2), read_weight.T, read_bias[None, :],
        read_out[None, :], layer_weight, layer_bias, norm_gain, norm_shift,
    )
    outs = (
        ((tiles, block, block), BF16), ((layers, padded, lanes), F32),
        ((8 * ((3 + 3 * layers + 7) // 8), lanes), F32), ((8, lanes), jnp.int32),
        ((layers + 2, lanes, lanes), BF16), ((plan.size,), jnp.int32),
    )
    keys = sum(plan.keys)
    turned, rel_rows, lane_rows, lane_heads, weights, order = pl.pallas_call(
        functools.partial(prep_kernel, plan, blocks, splits, layers),
        grid=(sum(steps),),
        in_specs=[SMEM] * 4
        + [whole(a.shape) for a in small]
        + [mask_spec(0, steps[0]), mask_spec(splits[0], steps[1]), mask_spec(splits[1], steps[2])],
        out_specs=[pl.BlockSpec((group, block, block), lambda i: (i, 0, 0))]
        + [whole(shape) for shape, _ in outs[1:5]]
        + [SMEM],
        out_shape=[jax.ShapeDtypeStruct(*o) for o in outs],
        scratch_shapes=[
            pltpu.VMEM((queries, width), F32),
            pltpu.SMEM((keys,), jnp.int32),
            pltpu.SMEM((keys,), jnp.int32),
            pltpu.SMEM((8,), jnp.int32),
        ],
        cost_estimate=pl.CostEstimate(
            flops=0, bytes_accessed=tiles * block * block * 6, transcendentals=0
        ),
        compiler_params=pltpu.CompilerParams(vmem_limit_bytes=16 << 20),
        name="prep",
    )(
        reg_blocks.T, hin_blocks.T, hout_blocks.T, query_head, *small, reg_mask, hin_mask, hout_mask,
    )

    def shifts(cells):
        left = lax.ppermute(cells, "ent", [(i, i + 1) for i in range(ends - 1)])
        right = lax.ppermute(cells, "ent", [(i + 1, i) for i in range(ends - 1)])
        return left, right

    def exchanged(part, strides):
        for stride in strides:
            part = part + lax.ppermute(part, "ent", [(i, i ^ stride) for i in range(ends)])
        return part

    far = [1 << i for i in range(1, ends.bit_length() - 1)]

    def call(kernel, name, operands, outs, scratch=(), tile_count=0, smem=1):
        return pl.pallas_call(
            kernel,
            in_specs=[SMEM] * smem + [VMEM] * (len(operands) - smem),
            out_specs=[VMEM] * len(outs),
            out_shape=outs,
            scratch_shapes=list(scratch),
            cost_estimate=pl.CostEstimate(
                flops=2 * tile_count * block * block * lanes,
                bytes_accessed=4 * tile_count * block * block,
                transcendentals=0,
            ),
            compiler_params=pltpu.CompilerParams(vmem_limit_bytes=16 << 20),
            name=name,
        )(*operands)

    state_shape = jax.ShapeDtypeStruct((ent_local, lanes), BF16)
    total_shape = jax.ShapeDtypeStruct((ent_local, lanes), F32)
    part_shape = jax.ShapeDtypeStruct((hubs, lanes), F32)
    hub_shape = jax.ShapeDtypeStruct((hubs, lanes), BF16)
    score_shape = jax.ShapeDtypeStruct((q_local, ent_local), F32)
    total_scratch = pltpu.VMEM((ent_local, lanes), F32)
    state_scratch = pltpu.VMEM((ent_local, lanes), BF16)
    tables = (order, turned, rel_rows)

    left, right = shifts(ent_feat)
    states, total, part = call(
        functools.partial(own_kernel, plan, 0), "own",
        tables + (ent_feat, lane_rows, lane_heads),
        (state_shape, total_shape, part_shape), (), tiles // 2,
    )
    hub_old = None
    hub_sum = None
    for layer in range(layers):
        last = layer == layers - 1
        if last:
            next_sum = exchanged(part, far + [1])
        elif layer == 0:
            part, left, right = lax.optimization_barrier((part, left, right))
            part = exchanged(part, [1])
        if layer > 0:
            old = () if layer == 1 else (hub_old,)
            total, hub_old = call(
                functools.partial(hout_kernel, plan, layer, layers), "hout",
                tables + (lane_rows, weights, total, hub_sum) + old, (total_shape, hub_shape), (), tiles // 4,
            )
            if not last:
                part, total = lax.optimization_barrier((part, total))
                part = exchanged(part, [1])
        (states,) = call(
            functools.partial(close_kernel, plan, layer, layers, width), "close",
            tables + (lane_rows, lane_heads, weights, total, states, left, right),
            (score_shape if last else state_shape,),
            (total_scratch,) + ((state_scratch, state_scratch) if layer == 0 else ()), tiles // 2,
        )
        if not last:
            states, part = lax.optimization_barrier((states, part))
            next_sum = exchanged(part, far)
        hub_sum = next_sum
        if not last:
            left, right = shifts(states)
            total, part = call(
                functools.partial(own_kernel, plan, layer + 1), "own",
                tables + (states,), (total_shape, part_shape), (), tiles // 2,
            )
    (hub_scores,) = call(
        functools.partial(hub_kernel, layers, width), "hubs",
        (lane_rows, weights, hub_sum, hub_old), (jax.ShapeDtypeStruct((q_local, HUB_DEV), F32),), smem=0,
    )
    scores = lax.all_to_all(states, "qry", split_axis=1, concat_axis=0, tiled=True)
    return scores, hub_scores


def solution(mesh):
    return jax.shard_map(
        body,
        mesh=mesh,
        in_specs=(
            P(None, "ent"), P(), P(), P(), P(), P(), P(), P(), P(),
            P("ent", None), P("ent"), P("ent", None, None),
            P("ent", None), P("ent"), P("ent", None, None),
            P("ent", None), P("ent"), P("ent", None, None),
            P(), P(), P(),
        ),
        out_specs=(P(None, ("ent", "qry")), P("qry", "ent")),
        check_vma=False,
    )
```

```python
import functools
import math

import jax
import jax.numpy as jnp
from jax import lax
from jax.experimental import pallas as pl
from jax.experimental.pallas import tpu as pltpu
from jax.sharding import PartitionSpec as P


HUB_DEV = 16
F32 = jnp.float32
BF16 = jnp.bfloat16
SMEM = pl.BlockSpec(memory_space=pltpu.SMEM)
VMEM = pl.BlockSpec(memory_space=pltpu.VMEM)
LEFT, OWN, RIGHT, HOUT, HIN = range(5)


class Plan:
    def __init__(self, counts, blocks, hub_blocks):
        reg, hin, hout = counts
        self.tiles = reg + hin + hout
        self.keys = [blocks, blocks, blocks, blocks, hub_blocks]
        mean = [reg / (3 * blocks)] * 3 + [hout / blocks, hin / hub_blocks]
        most = [reg] * 3 + [hout, hin]
        self.slots = [
            min(m + m % 2, 2 * math.ceil((a + 1.2 * math.sqrt(a)) / 2)) for a, m in zip(mean, most)
        ]
        self.first_key = [sum(self.keys[:s]) for s in range(5)]
        place = 16
        self.main = []
        for side in range(5):
            self.main.append(place)
            place += self.keys[side] * self.slots[side]
        self.more = []
        for side in range(5):
            self.more.append(place)
            place += most[side]
        self.size = place


def spreader(width, lanes, transposed=False):
    shape = (lanes, width) if transposed else (width, lanes)
    row = lax.broadcasted_iota(jnp.int32, shape, 0)
    column = lax.broadcasted_iota(jnp.int32, shape, 1)
    hit = lax.rem(row, width) == column if transposed else lax.rem(column, width) == row
    return hit.astype(F32).astype(BF16)


def contract_last(a, b):
    return lax.dot_general(a, b, (((1,), (1,)), ((), ())), preferred_element_type=F32)


def prep_kernel(plan, blocks, layers, *refs):
    count = 20
    sources, refs = refs[:count], refs[count:]
    turned, rel_rows, lane_rows, lane_heads, weights, order = refs[:6]
    landed = refs[6 : 6 + count]
    stack, q_rows, count_of, used, sems = refs[6 + count :]
    copies = [pltpu.make_async_copy(a, b, sems.at[i]) for i, (a, b) in enumerate(zip(sources, landed))]
    for copy in copies:
        copy.start()
    (
        reg_blocks, hin_blocks, hout_blocks, query_head, query_rel, reg_rel, hin_rel, hout_rel,
        query_table, rel_table, read_weight, read_bias, read_out, layer_weight, layer_bias, norm_gain,
        norm_shift, *masks,
    ) = landed
    width, relations = query_table.shape
    lanes = lane_rows.shape[1]
    q_local = lanes // width
    block = turned.shape[1]
    queries = query_rel.shape[1]
    first_block = lax.axis_index("ent") * blocks
    query_first = lax.axis_index("qry") * q_local
    empty = plan.tiles

    for key in range(sum(plan.keys)):
        count_of[key] = 0
    for side in range(5):
        used[side] = 0

    def clear(i, _):
        order[i] = empty
        return 0

    lax.fori_loop(plan.main[0], plan.more[0], clear, 0, unroll=8)
    spread = spreader(width, lanes)
    spread_back = spreader(width, lanes, True)
    same = lax.div(lax.broadcasted_iota(jnp.int32, (lanes, lanes), 0), width) == lax.div(
        lax.broadcasted_iota(jnp.int32, (lanes, lanes), 1), width
    )
    weights[2 * layers + 1] = jnp.where(same, 1.0 / width, 0.0).astype(BF16)
    for copy in copies[:17]:
        copy.wait()

    def picked(table, ids):
        row = lax.broadcasted_iota(jnp.int32, (relations, ids.shape[1]), 0)
        hit = (row == ids[...]).astype(F32).astype(BF16)
        return jnp.transpose(jnp.dot(table, hit, preferred_element_type=F32)).astype(BF16)

    base = 0
    for ids in (reg_rel, hin_rel, hout_rel):
        rows = picked(rel_table[...].reshape(layers * width, relations), ids)
        for layer in range(layers):
            rel_rows[layer, base : base + ids.shape[1], :] = jnp.dot(
                rows[:, layer * width : (layer + 1) * width], spread, preferred_element_type=F32
            )
        base += ids.shape[1]
    for layer in range(layers):
        rel_rows[layer, base:, :] = jnp.zeros((rel_rows.shape[1] - base, lanes), F32)

    def centred(rows):
        return rows - jnp.mean(rows, axis=1, keepdims=True)

    q_rows[...] = picked(query_table[...], query_rel).astype(F32)
    own = q_rows[...].astype(BF16)
    stack[...] = jnp.zeros_like(stack)
    stack[0:queries, :] = contract_last(own, read_weight[:, width:]) + read_bias[...]
    for at, rows in ((1, layer_bias), (1 + layers, norm_gain), (1 + 2 * layers, norm_shift)):
        values = centred(rows[...]) if at == 1 else rows[...]
        stack[queries + at : queries + at + layers, :] = values
    stack[queries : queries + 1, :] = read_out[...]
    wide = jnp.dot(stack[...], spread.astype(F32), precision=lax.Precision.HIGHEST)
    q_of_lane = lax.div(lax.broadcasted_iota(jnp.int32, (1, lanes), 1), width)
    wide_q = jnp.dot(own, spread, preferred_element_type=F32)
    mine = lax.broadcasted_iota(jnp.int32, wide_q.shape, 0) - query_first == q_of_lane
    lane_rows[...] = jnp.zeros_like(lane_rows)
    lane_rows[0:1, :] = jnp.sum(jnp.where(mine, wide_q, 0.0), axis=0, keepdims=True)
    lane_rows[1:2, :] = jnp.sum(jnp.where(mine, wide[:queries], 0.0), axis=0, keepdims=True)
    lane_rows[2 : 3 + 3 * layers, :] = wide[queries : queries + 1 + 3 * layers]
    lane_head = jnp.zeros((1, lanes), jnp.int32)
    for q in range(q_local):
        lane_head = jnp.where(q_of_lane == q, query_head[query_first + q], lane_head)
    lane_heads[...] = jnp.broadcast_to(lane_head, lane_heads.shape)

    def put_weight(at, tall):
        full = jnp.dot(tall.astype(BF16), spread, preferred_element_type=F32)
        weights[at] = jnp.where(same, full, 0.0).astype(BF16)

    for layer in range(layers):
        level = centred(layer_weight[layer].astype(F32))
        high = level.astype(BF16)
        low = (level - high.astype(F32)).astype(BF16)
        for part, value in enumerate((high, low)):
            put_weight(2 * layer + part, jnp.dot(spread_back, value, preferred_element_type=F32))
    put_weight(2 * layers, contract_last(spread_back, read_weight[:, :width]))

    eye = lax.broadcasted_iota(jnp.int32, (block, block), 0) == lax.broadcasted_iota(
        jnp.int32, (block, block), 1
    )
    eye = eye.astype(F32).astype(BF16)

    def note(tile, side, local, source, slots, main, more, key):
        seen = count_of[key]
        count_of[key] = seen + 1
        rest = used[side]
        fits = seen < slots
        used[side] = rest + jnp.where(fits, 0, 1)
        order[jnp.where(fits, main + local * slots + seen, more + rest)] = (
            tile + source * 4096 + local * (1 << 21)
        )

    def note_reg(t, tile):
        place = reg_blocks[1, t] - first_block + blocks
        side = lax.div(place, blocks)
        local = reg_blocks[0, t] - first_block
        note(
            tile, side, local, place - side * blocks, plan.slots[0],
            plan.main[0] + side * (plan.main[1] - plan.main[0]),
            plan.more[0] + side * (plan.more[1] - plan.more[0]), side * blocks + local,
        )

    def note_hin(t, tile):
        local = hin_blocks[0, t]
        note(
            tile, HIN, local, hin_blocks[1, t] - first_block, plan.slots[HIN], plan.main[HIN],
            plan.more[HIN], plan.first_key[HIN] + local,
        )

    def note_hout(t, tile):
        local = hout_blocks[0, t] - first_block
        note(
            tile, HOUT, local, hout_blocks[1, t], plan.slots[HOUT], plan.main[HOUT],
            plan.more[HOUT], plan.first_key[HOUT] + local,
        )

    base = 0
    for copy, mask, put in zip(copies[17:], masks, (note_reg, note_hin, note_hout)):
        copy.wait()
        count = mask.shape[0]
        group = math.gcd(count, 8)

        def turn(g, _, mask=mask, put=put, base=base, group=group):
            for u in range(group):
                t = g * group + u
                turned[base + t] = contract_last(eye, mask[t].astype(F32).astype(BF16)).astype(BF16)
                put(t, base + t)
            return 0

        lax.fori_loop(0, count // group, turn, 0)
        base += count
    for side in range(5):
        order[side] = used[side]


def slot_product(plan, layer, order, turned, rel_rows, places):
    block = turned.shape[1]
    lanes = rel_rows.shape[2]
    masks, values = [], []
    for place, source in places:
        word = order[place]
        tile = word & 4095
        start = pl.multiple_of(((word >> 12) & 511) * block, block)
        row = jnp.broadcast_to(rel_rows[layer, pl.ds(tile, 1), :], (16, lanes)).astype(BF16)
        value = source[pl.ds(start, block), :].reshape(block // 16, 16, lanes)
        values.append((value * row[None]).reshape(block, lanes))
        masks.append(turned[jnp.where(tile == plan.tiles, 0, tile)])
    return jnp.dot(
        jnp.concatenate(masks, axis=1), jnp.concatenate(values, axis=0), preferred_element_type=F32
    )


def key_product(plan, layer, side_sources, key, order, turned, rel_rows):
    total = None
    for side, source in side_sources:
        slots = plan.slots[side]
        for start in range(0, slots, 6):
            places = [
                (plan.main[side] + key * slots + u, source) for u in range(start, min(start + 6, slots))
            ]
            product = slot_product(plan, layer, order, turned, rel_rows, places)
            total = product if total is None else total + product
    return total


def add_rest(plan, layer, side, source, order, turned, rel_rows, total):
    block = turned.shape[1]

    def one(i, _):
        at = plan.more[side] + i
        place = pl.ds(pl.multiple_of((order[at] >> 21) * block, block), block)
        total[place, :] += slot_product(plan, layer, order, turned, rel_rows, [(at, source)])
        return 0

    lax.fori_loop(0, order[side], one, 0)


def normed_step(inputs, layer, layers, weights, lane_rows):
    bias, gain, shift = (lane_rows[3 + layer + i * layers : 4 + layer + i * layers, :] for i in range(3))
    centered = (
        jnp.dot(inputs, weights[2 * layer], preferred_element_type=F32)
        + jnp.dot(inputs, weights[2 * layer + 1], preferred_element_type=F32)
        + bias
    )
    squares = (centered * centered).astype(BF16)
    variance = jnp.dot(squares, weights[2 * layers + 1], preferred_element_type=F32)
    return jnp.maximum(centered * lax.rsqrt(variance + 1e-05) * gain + shift, 0.0)


def hit_lanes(rows, first, heads, values):
    place = first + lax.broadcasted_iota(jnp.int32, (rows, heads.shape[1]), 0)
    return jnp.where(place == heads, values, 0.0)


def first_states(feat, first, block, lane_rows, lane_heads, out):
    width, count = feat.shape
    columns = jnp.transpose(feat[...].astype(F32)).astype(BF16)
    spread = spreader(width, out.shape[1])
    for start in range(0, count, block):
        wide = jnp.dot(columns[start : start + block, :], spread, preferred_element_type=F32)
        hits = hit_lanes(block, first + start, lane_heads[0:1, :], lane_rows[0:1, :])
        out[start : start + block, :] = (wide + hits).astype(BF16)


def own_kernel(plan, layer, order, turned, rel_rows, *refs):
    block = turned.shape[1]
    if layer == 0:
        feat, lane_rows, lane_heads, states, total, hub_part = refs
        first = lax.axis_index("ent") * feat.shape[1]
        first_states(feat, first, block, lane_rows, lane_heads, states)
    else:
        states, total, hub_part = refs
    for side, out in ((HIN, hub_part), (OWN, total)):
        for key in range(plan.keys[side]):
            out[key * block : (key + 1) * block, :] = key_product(
                plan, layer, ((side, states),), key, order, turned, rel_rows
            )
        add_rest(plan, layer, side, states, order, turned, rel_rows, out)


def side_kernel(block, left_feat, right_feat, lane_rows, lane_heads, left, right):
    count = left_feat.shape[1]
    first = lax.axis_index("ent") * count
    first_states(left_feat, first - count, block, lane_rows, lane_heads, left)
    first_states(right_feat, first + count, block, lane_rows, lane_heads, right)


def update_hubs(hub_sum, hub_old, layer, layers, weights, lane_rows):
    inputs = (hub_sum * lane_rows[0:1, :]).astype(BF16)
    grown = normed_step(inputs, layer, layers, weights, lane_rows)
    if hub_old is not None:
        grown = grown + hub_old.astype(F32)
    return grown.astype(BF16)


def hout_kernel(plan, layer, layers, order, turned, rel_rows, lane_rows, weights, total_in, hub_sum, *refs):
    block = turned.shape[1]
    if layer == 1:
        total, hub_new = refs
        hub_old = None
    else:
        old, total, hub_new = refs
        hub_old = old[...]
    hub_new[...] = update_hubs(hub_sum[...], hub_old, layer - 1, layers, weights, lane_rows)
    for key in range(plan.keys[HOUT]):
        place = slice(key * block, (key + 1) * block)
        total[place, :] = total_in[place, :] + key_product(
            plan, layer, ((HOUT, hub_new),), key, order, turned, rel_rows
        )
    add_rest(plan, layer, HOUT, hub_new, order, turned, rel_rows, total)


def score_rows(values, width, layers, weights, lane_rows):
    lanes = values.shape[1]
    row = lax.broadcasted_iota(jnp.int32, (8, lanes), 0)
    column = lax.broadcasted_iota(jnp.int32, (8, lanes), 1)
    picks = jnp.where(lax.div(column, width) == row, lane_rows[2:3, :], 0.0)
    features = jnp.dot(values, weights[2 * layers], preferred_element_type=F32) + lane_rows[1:2, :]
    features = jnp.maximum(features, 0.0)
    high = features.astype(BF16)
    low = (features - high.astype(F32)).astype(BF16)
    pick_high = picks.astype(BF16)
    pick_low = (picks - pick_high.astype(F32)).astype(BF16)
    return contract_last(pick_high, high) + contract_last(pick_high, low) + contract_last(pick_low, high)


def close_kernel(plan, layer, layers, width, order, turned, rel_rows, lane_rows, lane_heads, weights, total_in, own, *refs):
    last = layer == layers - 1
    count = own.shape[0]
    block = turned.shape[1]
    first = lax.axis_index("ent") * count
    left, right, out, total = refs
    total[...] = total_in[...]
    add_rest(plan, layer, LEFT, left, order, turned, rel_rows, total)
    add_rest(plan, layer, RIGHT, right, order, turned, rel_rows, total)
    lane_q = lane_rows[0:1, :]
    for key in range(plan.keys[LEFT]):
        place = slice(key * block, (key + 1) * block)
        sums = total[place, :] + key_product(
            plan, layer, ((LEFT, left), (RIGHT, right)), key, order, turned, rel_rows
        )
        hits = hit_lanes(block, first + key * block, lane_heads[0:1, :], lane_q)
        inputs = (sums * lane_q + hits).astype(BF16)
        grown = normed_step(inputs, layer, layers, weights, lane_rows)
        new = (grown + own[place, :].astype(F32)).astype(BF16)
        if last:
            out[:, place] = score_rows(new, width, layers, weights, lane_rows)[: out.shape[0]]
        else:
            out[place, :] = new


def hub_kernel(layers, width, lane_rows, weights, hub_sum, hub_old, out):
    mine = out.shape[1]
    place = pl.ds(pl.multiple_of(lax.axis_index("ent") * mine, mine), mine)
    new = update_hubs(hub_sum[place, :], hub_old[place, :], layers - 1, layers, weights, lane_rows)
    out[...] = score_rows(new, width, layers, weights, lane_rows)[: out.shape[0]]


def body(
    ent_feat, query_head, query_rel, query_table, rel_table, layer_weight, layer_bias, norm_gain,
    norm_shift, reg_blocks, reg_rel, reg_mask, hin_blocks, hin_rel, hin_mask, hout_blocks,
    hout_rel, hout_mask, read_weight, read_bias, read_out,
):
    ends = lax.axis_size("ent")
    layers = rel_table.shape[0]
    q_local = query_head.shape[0] // lax.axis_size("qry")
    width, ent_local = ent_feat.shape
    block = reg_mask.shape[1]
    blocks = ent_local // block
    hubs = HUB_DEV * ends
    lanes = q_local * width
    counts = [reg_mask.shape[0], hin_mask.shape[0], hout_mask.shape[0]]
    tiles = sum(counts)
    plan = Plan(counts, blocks, hubs // block)
    padded = tiles + 8
    queries = query_head.shape[0]

    given = (
        reg_blocks.T, hin_blocks.T, hout_blocks.T, query_head,
        query_rel[None, :], reg_rel[None, :], hin_rel[None, :], hout_rel[None, :],
        query_table.T, jnp.swapaxes(rel_table, 1, 2), read_weight.T, read_bias[None, :],
        read_out[None, :], layer_weight, layer_bias, norm_gain, norm_shift,
        reg_mask, hin_mask, hout_mask,
    )
    outs = (
        ((tiles, block, block), BF16), ((layers, padded, lanes), F32),
        ((8 * ((3 + 3 * layers + 7) // 8), lanes), F32), ((8, lanes), jnp.int32),
        ((2 * layers + 2, lanes, lanes), BF16), ((plan.size,), jnp.int32),
    )
    stack_rows = queries + 8 * ((1 + 3 * layers + 7) // 8)
    turned, rel_rows, lane_rows, lane_heads, weights, order = pl.pallas_call(
        functools.partial(prep_kernel, plan, blocks, layers),
        in_specs=[pl.BlockSpec(memory_space=pltpu.HBM)] * len(given),
        out_specs=[VMEM] * 5 + [SMEM],
        out_shape=[jax.ShapeDtypeStruct(*o) for o in outs],
        scratch_shapes=[
            (pltpu.SMEM if i < 4 else pltpu.VMEM)(a.shape, a.dtype) for i, a in enumerate(given)
        ]
        + [
            pltpu.VMEM((stack_rows, width), F32),
            pltpu.VMEM((queries, width), F32),
            pltpu.SMEM((sum(plan.keys),), jnp.int32),
            pltpu.SMEM((8,), jnp.int32),
            pltpu.SemaphoreType.DMA((len(given),)),
        ],
        cost_estimate=pl.CostEstimate(
            flops=0, bytes_accessed=tiles * block * block * 6, transcendentals=0
        ),
        compiler_params=pltpu.CompilerParams(vmem_limit_bytes=24 << 20),
        name="prep",
    )(*(pltpu.with_memory_space_constraint(a, pltpu.HBM) for a in given))

    def shifts(cells):
        left = lax.ppermute(cells, "ent", [(i, i + 1) for i in range(ends - 1)])
        right = lax.ppermute(cells, "ent", [(i + 1, i) for i in range(ends - 1)])
        return left, right

    def exchanged(part, strides):
        for stride in strides:
            got = lax.ppermute(part, "ent", [(i, i ^ stride) for i in range(ends)])
            part = part + got
        return part

    far = [1 << i for i in range(1, ends.bit_length() - 1)]

    def call(kernel, operands, outs, scratch=(), tile_count=0, smem=1):
        return pl.pallas_call(
            kernel,
            in_specs=[SMEM] * smem + [VMEM] * (len(operands) - smem),
            out_specs=[VMEM] * len(outs),
            out_shape=outs,
            scratch_shapes=list(scratch),
            cost_estimate=pl.CostEstimate(
                flops=2 * tile_count * block * block * lanes,
                bytes_accessed=4 * tile_count * block * block,
                transcendentals=0,
            ),
            compiler_params=pltpu.CompilerParams(vmem_limit_bytes=16 << 20),
        )(*operands)

    state_shape = jax.ShapeDtypeStruct((ent_local, lanes), BF16)
    total_shape = jax.ShapeDtypeStruct((ent_local, lanes), F32)
    part_shape = jax.ShapeDtypeStruct((hubs, lanes), F32)
    hub_shape = jax.ShapeDtypeStruct((hubs, lanes), BF16)
    score_shape = jax.ShapeDtypeStruct((q_local, ent_local), F32)
    total_scratch = pltpu.VMEM((ent_local, lanes), F32)
    state_scratch = pltpu.VMEM((ent_local, lanes), BF16)
    tables = (order, turned, rel_rows)

    left, right = shifts(ent_feat)
    states, total, part = call(
        functools.partial(own_kernel, plan, 0),
        tables + (ent_feat, lane_rows, lane_heads),
        (state_shape, total_shape, part_shape), (), tiles // 2,
    )
    part, left, right = lax.optimization_barrier((part, left, right))
    part = exchanged(part, [1])
    left, right = call(
        functools.partial(side_kernel, block),
        (left, right, lane_rows, lane_heads), (state_shape, state_shape), (), tiles // 8, smem=0,
    )
    part, left, right = lax.optimization_barrier((part, left, right))
    part = exchanged(part, far[:1])

    def close(layer, total, states, left, right):
        last = layer == layers - 1
        (new,) = call(
            functools.partial(close_kernel, plan, layer, layers, width),
            tables + (lane_rows, lane_heads, weights, total, states, left, right),
            (score_shape if last else state_shape,), (total_scratch,), tiles // 2,
        )
        return new

    states = close(0, total, states, left, right)
    hub_old = None
    for layer in range(1, layers):
        last = layer == layers - 1
        states, part = lax.optimization_barrier((states, part))
        left, right = shifts(states)
        hub_sum = exchanged(part, far[1:]) if layer == 1 else part
        total, part = call(
            functools.partial(own_kernel, plan, layer),
            tables + (states,), (total_shape, part_shape), (), tiles // 2,
        )
        old = () if layer == 1 else (hub_old,)
        total, hub_old = call(
            functools.partial(hout_kernel, plan, layer, layers),
            tables + (lane_rows, weights, total, hub_sum) + old, (total_shape, hub_shape), (), tiles // 4,
        )
        part, total = lax.optimization_barrier((part, total))
        part = exchanged(part, far + [1])
        states = close(layer, total, states, left, right)
    hub_sum = part
    (hub_scores,) = call(
        functools.partial(hub_kernel, layers, width),
        (lane_rows, weights, hub_sum, hub_old), (jax.ShapeDtypeStruct((q_local, HUB_DEV), F32),), smem=0,
    )
    scores = lax.all_to_all(states, "qry", split_axis=1, concat_axis=0, tiled=True)
    return scores, hub_scores


def solution(mesh):
    return jax.shard_map(
        body,
        mesh=mesh,
        in_specs=(
            P(None, "ent"), P(), P(), P(), P(), P(), P(), P(), P(),
            P("ent", None), P("ent"), P("ent", None, None),
            P("ent", None), P("ent"), P("ent", None, None),
            P("ent", None), P("ent"), P("ent", None, None),
            P(), P(), P(),
        ),
        out_specs=(P(None, ("ent", "qry")), P("qry", "ent")),
        check_vma=False,
    )
```
